32 devices in a mesh: grp: 2 (over y), sp: 4 (over z), fs: 2 (over x), hd: 2 (over core).
Axes of the slice: x: 2, y: 2, z: 4, core: 2. Of those that a mesh axis runs over, the one named last changes fastest.
Arguments:
- queries: bfloat16 [4, 3, 16, 16, 2560], P(('grp', 'fs'), None, 'sp', None, 'hd'), parts along dimension 0, may hold values from -6 to 6
- keys: bfloat16 [4, 3, 16, 16, 2560], P(('grp', 'fs'), None, 'sp', None, 'hd'), parts along dimension 0, may hold values from -6 to 6
- values: bfloat16 [4, 3, 16, 16, 2560], P(('grp', 'fs'), None, 'sp', None, 'hd'), parts along dimension 0, may hold values from -6 to 6
- windows: int32 [20, 2], P('hd'), may hold values from 0 to 1, as said below
- row_mask: int32 [16], replicated, may hold values from 0 to 1, as said below
- out_weight: bfloat16 [2560, 5120], P('hd', 'fs'), may hold values from -0.5 to 0.5
Outputs:
- projected: bfloat16 [4, 3, 16, 16, 5120], P(('grp', 'fs'), None, 'sp', None, 'hd'), parts along dimension 0
The draws below stay inside these ranges and needn't reach their ends.
There are 2 independent parts, one for each index of `grp`. The reference program is written for one: setup_inputs(seed, part) draws one part's arguments, and reference() takes and returns one part's arrays. A program takes and returns all parts, laid end to end along the dimension named above; an argument that names none is the same for every part. Nothing has to cross between parts.
Inputs may be any that keep to these rules, and one draw needn't show every extreme that they name: windows[h, 0] and windows[h, 1] are head h's reach in tiles along height and width; each column holds a 1. `row_mask`: the last row is padded.
All inputs are finite; a program needn't handle non-finite values.
Results may differ from the reference program's by a relative error of at most 0.0052.
Values may be sent and summed in bfloat16 or wider, within the bound.
No kernel may reach another device: no remote copies, remote signals or barrier semaphores. Data moves between devices by JAX's collectives and lax.ppermute only.
A program may use at most 64 MiB of HBM per device.

```python
import math
import jax
import jax.numpy as jnp
from jax import lax

D = 5120
HEAD_DIM = 128
HEADS = 20
FRAMES = 3
TILE_H = 5
TILE_W = 8
COLS = 16
ROWS_DEV = 4
VIDEOS = 2
H_PAD = 16


def draw_queries(key, part):
    full_shape = (VIDEOS, FRAMES, H_PAD, COLS, HEADS * HEAD_DIM)
    return jnp.clip(1.4 * jax.random.normal(jax.random.fold_in(key, 1), full_shape, jnp.float32), -6.0, 6.0).astype(jnp.bfloat16)


def draw_keys(key, part):
    full_shape = (VIDEOS, FRAMES, H_PAD, COLS, HEADS * HEAD_DIM)
    return jnp.clip(1.4 * jax.random.normal(jax.random.fold_in(key, 2), full_shape, jnp.float32), -6.0, 6.0).astype(jnp.bfloat16)


def draw_windows(key, part):
    reaches = jax.random.randint(jax.random.fold_in(key, 21), (HEADS, 2), 0, 2)
    forced_heads = jax.random.randint(jax.random.fold_in(key, 22), (2,), 0, HEADS)
    return jnp.where(jnp.arange(HEADS)[:, None] == forced_heads[None, :], 1, reaches).astype(jnp.int32)


def draw_row_mask(key, part):
    row_ids = jnp.arange(H_PAD)
    steady_start = max(H_PAD - 4 * ROWS_DEV, 4)
    coins = jax.random.randint(jax.random.fold_in(key, 31), (H_PAD,), 0, 2)
    valid = jnp.where(row_ids >= steady_start, 1, coins)
    return jnp.where(row_ids == H_PAD - 1, 0, valid).astype(jnp.int32)


def shard_levels(stream_key, shape, split, least, top_value):
    level, own = 1.0, jax.random.fold_in(stream_key, 6)
    for axis_at, parts in split:
        heights = jnp.exp(jax.random.uniform(jax.random.fold_in(own, axis_at), (parts,), jnp.float32, least / len(split), top_value / len(split)))
        level = level * jnp.repeat(heights, shape[axis_at] // parts).reshape([-1 if axis == axis_at else 1 for axis in range(len(shape))])
    return level


def gaussian(rng, dims, spread, most, shards=(), kind=jnp.bfloat16):
    values = spread * jax.random.normal(rng, dims, jnp.float32)
    if shards:
        values = values * shard_levels(rng, dims, shards, -0.22, 0.18)
    return jnp.clip(values, -most, most).astype(kind)


def setup_inputs(seed: int = 0, part: int = 0) -> dict:
    arg_keys = jax.random.split(jax.random.key(seed), 7)
    part_splits = jax.random.split(jax.random.fold_in(arg_keys[6], part), 7)
    return {
        "queries": draw_queries(jax.random.fold_in(jax.random.fold_in(arg_keys[6], part), 71), part),
        "keys": draw_keys(jax.random.fold_in(jax.random.fold_in(arg_keys[6], part), 71), part),
        "values": gaussian(part_splits[2], (VIDEOS, FRAMES, H_PAD, COLS, HEADS * HEAD_DIM), 1.0, 6.0, ((0, 2), (2, 4), (4, 2))),
        "windows": draw_windows(jax.random.fold_in(arg_keys[6], 71), part),
        "row_mask": draw_row_mask(jax.random.fold_in(arg_keys[6], 71), part),
        "out_weight": gaussian(arg_keys[5], (HEADS * HEAD_DIM, D), (HEADS * HEAD_DIM // 16) ** -0.5, 0.5, ((0, 2), (1, 2))),
    }


def reference(queries, keys, values, windows, row_mask, out_weight):
    video_count, frame_count, row_count, col_count, feature_count = queries.shape
    tile_count = -(-row_count // TILE_H)
    tail_rows = tile_count * TILE_H - row_count

    def spread_heads(source):
        shaped = source.astype(jnp.float32).reshape(video_count, frame_count, row_count, col_count, HEADS, HEAD_DIM)
        return jnp.pad(shaped, ((0, 0), (0, 0), (TILE_H, 2 * TILE_H + tail_rows), (0, 0), (0, 0), (0, 0)))
    query_pad = spread_heads(queries)
    key_pad = spread_heads(keys)
    value_pad = spread_heads(values)
    valid_pad = jnp.pad(row_mask, (TILE_H, 2 * TILE_H + tail_rows)) == 1
    col_tiles = jnp.arange(col_count, dtype=jnp.int32) // TILE_W
    col_gap = jnp.abs(col_tiles[:, None] - col_tiles[None, :])
    row_gap = jnp.abs(jnp.arange(3 * TILE_H, dtype=jnp.int32) // TILE_H - 1)
    score_scale = 1.0 / math.sqrt(HEAD_DIM)

    def one_tile(tile_index):
        start_query = ((tile_index + 1) * TILE_H).astype(jnp.int32)
        start_key = (tile_index * TILE_H).astype(jnp.int32)
        query_block = lax.dynamic_slice_in_dim(query_pad, start_query, TILE_H, 2)
        key_block = lax.dynamic_slice_in_dim(key_pad, start_key, 3 * TILE_H, 2)
        value_block = lax.dynamic_slice_in_dim(value_pad, start_key, 3 * TILE_H, 2)
        key_ok = lax.dynamic_slice_in_dim(valid_pad, start_key, 3 * TILE_H, 0)
        query_ok = lax.dynamic_slice_in_dim(valid_pad, start_query, TILE_H, 0)
        allowed = (row_gap[None, None, :, None] <= windows[:, 0][:, None, None, None]) & (col_gap[None, :, None, :] <= windows[:, 1][:, None, None, None]) & key_ok[None, None, :, None]
        scores = jnp.einsum('vfrchd,vgkehd->vhfrcgke', query_block, key_block, precision=lax.Precision.HIGHEST) * score_scale
        mask_full = allowed[None, :, None, None, :, None, :, :]
        row_peak = lax.optimization_barrier(jnp.max(jnp.where(mask_full, scores, -1e+30), axis=(5, 6, 7), keepdims=True))
        exponent = jnp.where(mask_full, jnp.exp(scores - row_peak), 0.0)
        totals = lax.optimization_barrier(jnp.sum(exponent, axis=(5, 6, 7)))
        weights16 = lax.optimization_barrier(exponent.astype(jnp.bfloat16)).astype(jnp.float32)
        mixed = jnp.einsum('vhfrcgke,vgkehd->vfrchd', weights16, value_block, precision=lax.Precision.HIGHEST)
        totals_moved = jnp.transpose(totals, (0, 2, 3, 4, 1))
        keep_rows = query_ok[None, None, :, None, None]
        attention = jnp.where(keep_rows[..., None], mixed / jnp.where(keep_rows, totals_moved, 1.0)[..., None], 0.0)
        return attention.astype(jnp.bfloat16)
    blocks = lax.map(one_tile, jnp.arange(tile_count, dtype=jnp.int32))
    joined = jnp.transpose(blocks, (1, 2, 0, 3, 4, 5, 6)).reshape(video_count, frame_count, tile_count * TILE_H, col_count, HEADS * HEAD_DIM)[:, :, :row_count]
    flattened = joined.reshape(-1, HEADS * HEAD_DIM)
    projected = jnp.dot(flattened, out_weight, preferred_element_type=jnp.float32).astype(jnp.bfloat16)
    return projected.reshape(video_count, frame_count, row_count, col_count, -1)
```

```python
import functools
import math

import jax
import jax.numpy as jnp
from jax import lax
from jax.experimental import pallas as pl
from jax.experimental.pallas import tpu as pltpu
from jax.sharding import PartitionSpec as P

TILE_H = 5
TILE_W = 8
CHUNKS = 5


def reach_plan(devices, rows):
    total = devices * rows
    needs = []
    for i in range(devices):
        first, last = i * rows, (i + 1) * rows - 1
        low = max((first // TILE_H - 1) * TILE_H, 0)
        high = min((last // TILE_H + 2) * TILE_H, total) - 1
        needs.append({b - i for b in range(low // rows, high // rows + 1)})
    farthest = max(abs(d) for need in needs for d in need)
    slots = [[0]]
    for d in range(1, farthest + 1):
        if any(-d in need and d in need for need in needs):
            slots += [[-d], [d]]
        else:
            slots.append([-d, d])
    return slots, farthest


def shift(block, axis, distance):
    devices = lax.axis_size(axis)
    route = [(i - distance, i) for i in range(devices) if 0 <= i - distance < devices]
    return lax.ppermute(block, axis, route)


def attention_kernel(slots, heads, size, scale, at_ref, reach_ref, code_ref, valid_ref, q_ref, k_ref, v_ref, *rest):
    blocks, out_ref = rest[:-1], rest[-1]
    by_distance = {}
    order = [d for slot in slots for d in slot if d != 0]
    for d, ref in zip(order, blocks):
        by_distance[d] = ref
    tokens = math.prod(q_ref.shape[:-1])
    code = code_ref[...]
    plane = code.shape[0]
    frames = tokens // plane
    for head in range(heads):
        columns = slice(head * size, (head + 1) * size)
        keys, values = [], []
        for slot in slots:
            for part, own, gathered in ((0, k_ref, keys), (1, v_ref, values)):
                picks = []
                for d in slot:
                    ref = own if d == 0 else by_distance[d].at[part]
                    picks.append(ref[..., columns].reshape(tokens, size))
                pick = picks[0]
                if len(slot) == 2:
                    pick = jnp.where(at_ref[slots.index(slot)] == slot[0], picks[0], picks[1])
                gathered.append(pick)
        key = jnp.concatenate(keys, axis=0)
        value = jnp.concatenate(values, axis=0)
        query = q_ref[..., columns].reshape(tokens, size)
        scores = lax.dot_general(query, key, (((1,), (1,)), ((), ())), preferred_element_type=jnp.float32)
        blocked = (code & reach_ref[head]) != 0
        scores = scores.reshape(frames, plane, scores.shape[-1])
        scores = jnp.where(blocked[None], -1e30, scores * scale)
        peak = jnp.max(scores, axis=-1, keepdims=True)
        expo = jnp.exp(scores - peak)
        total = jnp.sum(expo, axis=-1, keepdims=True)
        weights = expo.astype(jnp.bfloat16).reshape(tokens, -1)
        mixed = jnp.dot(weights, value, preferred_element_type=jnp.float32).reshape(frames, plane, size)
        result = mixed * (valid_ref[...][None] / total)
        out_ref[:, columns] = result.reshape(tokens, size).astype(jnp.bfloat16)


def attend(slots, at, reach, code, valid, queries, keys, values, blocks, chunk, heads, size):
    lead = queries.shape[:-1]
    tokens = math.prod(lead)
    width = heads * size
    zeros = (0,) * len(lead)
    whole = pl.BlockSpec(memory_space=pltpu.VMEM)
    local = pl.BlockSpec(lead + (width,), lambda step, *_: zeros + (chunk,))
    scalar = pl.BlockSpec(memory_space=pltpu.SMEM)
    key_count = code.shape[1]
    return pl.pallas_call(
        functools.partial(attention_kernel, slots, heads, size, 1.0 / math.sqrt(size)),
        grid=(1,),
        out_shape=jax.ShapeDtypeStruct((tokens, width), jnp.bfloat16),
        in_specs=[scalar, scalar, whole, whole, local, local, local] + [whole] * len(blocks),
        out_specs=whole,
        cost_estimate=pl.CostEstimate(
            flops=4 * tokens * key_count * width,
            transcendentals=tokens * key_count * heads,
            bytes_accessed=2 * width * (2 * tokens + 2 * key_count),
        ),
        name="attend",
    )(at, reach, code, valid, queries, keys, values, *blocks)


def on_device(devices, groups, queries, keys, values, windows, row_mask, out_weight):
    frames, rows, cols, features = queries.shape[1:]
    heads = windows.shape[0]
    size = features // heads
    chunks = CHUNKS if heads % CHUNKS == 0 else 1
    per = heads // chunks
    width = per * size
    slots, farthest = reach_plan(devices, rows)
    here = lax.axis_index("sp")
    fs = lax.axis_index("fs")
    hd = lax.axis_index("hd")

    order = [d for slot in slots for d in slot if d != 0]
    moved = []
    for c in range(chunks):
        span = slice(c * width, (c + 1) * width)
        pair = jnp.stack([keys[..., span], values[..., span]])
        found = {}
        for sign in (1, -1):
            hop = pair
            for d in range(1, farthest + 1):
                hop = shift(hop, "sp", sign)
                found[-sign * d] = hop
        moved.append([found[d] for d in order])

    weight_other = lax.ppermute(out_weight, "hd", [(0, 1), (1, 0)])

    total_rows = devices * rows
    q_rows = here * rows + jnp.arange(rows)
    col_tiles = jnp.arange(cols) // TILE_W
    col_bit = jnp.where(col_tiles[:, None] == col_tiles[None, :], 0, 2)
    parts = []
    taken = []
    lowest = jnp.maximum((here * rows // TILE_H - 1) * TILE_H, 0)
    for slot in slots:
        d = jnp.int32(slot[0])
        if len(slot) == 2:
            d = jnp.where((here + slot[0] + 1) * rows - 1 >= lowest, d, slot[1])
        taken.append(d)
        k_rows = (here + d) * rows + jnp.arange(rows)
        inside = (k_rows >= 0) & (k_rows < total_rows)
        hit = k_rows[:, None] == jnp.arange(total_rows)[None, :]
        ok = inside & (jnp.sum(jnp.where(hit, row_mask[None, :], 0), axis=1) == 1)
        gap = jnp.abs(q_rows[:, None] // TILE_H - k_rows[None, :] // TILE_H)
        row_code = jnp.where(ok[None, :] & (gap <= 1), gap, 4)
        full = row_code[:, None, None, :, None] | col_bit[None, :, None, None, :]
        full = jnp.broadcast_to(full, (rows, cols, frames, rows, cols))
        parts.append(full.reshape(rows * cols, frames * rows * cols))
    code = jnp.concatenate(parts, axis=1).astype(jnp.int32)
    hit = q_rows[:, None] == jnp.arange(total_rows)[None, :]
    q_ok = jnp.sum(jnp.where(hit, row_mask[None, :], 0), axis=1) == 1
    valid = jnp.broadcast_to(q_ok[:, None, None], (rows, cols, 1)).reshape(rows * cols, 1).astype(jnp.float32)
    reach = 7 - jnp.where(windows[:, 0] >= 1, 1, 0) - jnp.where(windows[:, 1] >= 1, 2, 0)
    at = jnp.stack(taken)

    half = groups // 2
    tokens = frames * rows * cols
    total = None
    for c in range(chunks):
        mixed = attend(
            slots, at, reach[c * per : (c + 1) * per], code, valid, queries, keys, values, moved[c], c, per, size
        )
        pieces = []
        for t in range(groups):
            route = []
            for v in range(groups):
                for g in range(2):
                    to = (g * half + v % half + t) % groups
                    route.append((v * 2 + g, to * 2 + v // half))
            pieces.append(lax.ppermute(mixed, ("fs", "hd"), route))
        ordered = []
        for j in range(groups):
            which = (fs - j) % groups
            pick = pieces[0]
            for t in range(1, groups):
                pick = jnp.where(which == t, pieces[t], pick)
            ordered.append(pick)
        first = jnp.concatenate(ordered[:half], axis=0)
        second = jnp.concatenate(ordered[half:], axis=0)
        own = jnp.where(hd == 0, first, second)
        other = jnp.where(hd == 0, second, first)
        span = slice(c * width, (c + 1) * width)
        part = jnp.dot(own, out_weight[span], preferred_element_type=jnp.float32) + jnp.dot(
            other, weight_other[span], preferred_element_type=jnp.float32
        )
        total = part if total is None else total + part

    block = total.astype(jnp.bfloat16).reshape(half, tokens, -1)
    wide = block.shape[-1]
    result = []
    for t in range(half):
        send = block[0] if half == 1 else lax.dynamic_index_in_dim(block, (fs + t) % half, 0, keepdims=False)
        route = []
        for f in range(groups):
            for h in range(2):
                route.append((f * 2 + h, (h * half + (f + t) % half) * 2 + f // half))
        result.append(lax.ppermute(send, ("fs", "hd"), route))
    if half == 1:
        joined = result[0]
    else:
        placed = []
        for j in range(half):
            which = (fs - j) % half
            pick = result[0]
            for t in range(1, half):
                pick = jnp.where(which == t, result[t], pick)
            placed.append(pick)
        joined = jnp.concatenate(placed, axis=1)
    return joined.reshape(1, frames, rows, cols, -1)


def solution(mesh):
    return jax.shard_map(
        functools.partial(on_device, mesh.shape["sp"], mesh.shape["fs"]),
        mesh=mesh,
        in_specs=(
            P(("grp", "fs"), None, "sp", None, "hd"),
            P(("grp", "fs"), None, "sp", None, "hd"),
            P(("grp", "fs"), None, "sp", None, "hd"),
            P("hd", None),
            P(),
            P("hd", "fs"),
        ),
        out_specs=P(("grp", "fs"), None, "sp", None, "hd"),
        check_vma=False,
    )
```
